128 devices in a mesh: dst: 32 (over y, x, core), src: 4 (over z).
Axes of the slice: x: 4, y: 4, z: 4, core: 2. Of those that a mesh axis runs over, the one named last changes fastest.
Arguments:
- points: bfloat16 [16384, 256], P(('dst', 'src')), may hold values from -6 to 6
- w_query: bfloat16 [256, 256], replicated, may hold values from -16 to 16
- w_key: bfloat16 [256, 256], replicated, may hold values from -0.375 to 0.375
- w_value: bfloat16 [256, 256], replicated, may hold values from -0.375 to 0.375
- w_out: bfloat16 [256, 256], replicated, may hold values from -0.375 to 0.375
- gain: float32 [256], replicated, may hold values from 0.25 to 1.75
- cell_counts: int32 [32, 4], P('dst', 'src'), may hold values from 8 to 64, as said below
- tile_slots: int32 [32, 4, 64], P('dst', 'src'), may hold values from 0 to 127, as said below
- edge_masks: int32 [32, 4, 64, 128, 128], P('dst', 'src'), may hold values 0 or 1
Outputs:
- out_points: bfloat16 [16384, 256], P(('dst', 'src'))
The draws below stay inside these ranges and needn't reach their ends.
Inputs may be any that keep to these rules, and one draw needn't show every extreme that they name: `cell_counts`: the busiest cell lists exactly 64 tiles. `tile_slots`: within one cell the 64 tile numbers are all different.
All inputs are finite; a program needn't handle non-finite values. No bound on the sum of `edge_masks` on one device may be relied on, other than what follows from the above.
Results may differ from the reference program's by a relative error of at most 0.0085.
The reference program's roundings to bfloat16 on the way (of `tangent`, `queries` and `mixed`) count: a program that leaves them out, or rounds other values in their place, can miss the bound.
Values may be sent and summed in bfloat16 or wider, within the bound.
No kernel may reach another device: no remote copies, remote signals or barrier semaphores. Data moves between devices by JAX's collectives and lax.ppermute only.
A program may use at most 64 MiB of HBM per device.

```python
import math
import jax
import jax.numpy as jnp
from jax import lax

D = 256
HEADS = 4
TILE = 128
NODE_DEV = 128
NODES = 16384
TILES = 64
N_DST = 32
N_SRC = 4


def draw_w_query(key, part):
    base = jax.random.normal(key, (D, D), jnp.float32) * D ** (-0.5)
    return base.astype(jnp.bfloat16)


def draw_cell_counts(key, part):
    least_count = max(1, TILES // 8)
    counts = jax.random.randint(key, (N_DST * N_SRC,), least_count, TILES + 1, dtype=jnp.int32)
    busiest = jax.random.randint(jax.random.fold_in(key, 3), (), 0, N_DST * N_SRC, dtype=jnp.int32)
    counts = counts.at[busiest].set(TILES)
    return counts.reshape(N_DST, N_SRC)


def draw_tile_slots(key, part):
    grid_tiles = N_SRC * NODE_DEV // TILE * (N_DST * NODE_DEV // TILE)
    cell_keys = jax.random.split(key, N_DST * N_SRC)

    def one_cell(cell_key):
        return jax.random.permutation(cell_key, grid_tiles)[:TILES].astype(jnp.int32)
    return jax.vmap(one_cell)(cell_keys).reshape(N_DST, N_SRC, TILES)


def place_ends(drawn, stream_key, least, top_value):
    shape = drawn.shape
    index_at = [jax.random.randint(jax.random.fold_in(stream_key, axis), (), 0, shape[axis]) for axis in range(len(shape))]
    drawn = drawn.at[tuple(index_at)].set(least)
    longest = shape.index(max(shape))
    index_at[longest] = (index_at[longest] + 1) % shape[longest]
    return drawn.at[tuple(index_at)].set(top_value)


def block_levels(key, extent, cuts, least, top_value):
    def one(dim, blocks):
        heights = jax.random.uniform(jax.random.fold_in(jax.random.fold_in(key, 6), dim), (blocks,), jnp.float32, least / len(cuts), top_value / len(cuts))
        return jnp.repeat(jnp.exp(heights), extent[dim] // blocks).reshape((-1,) + (1,) * (len(extent) - dim - 1))

    level = one(*cuts[0])
    for cut in cuts[1:]:
        level = level * one(*cut)
    return level


def scatter_about(rng, dims, spread, most, pieces=(), held_as=jnp.bfloat16):
    values = jax.random.normal(rng, dims, jnp.float32) * spread
    if len(pieces) > 0:
        values = block_levels(rng, dims, pieces, -0.22, 0.18) * values
    return jnp.clip(values, min=-most, max=most).astype(held_as)


def setup_inputs(seed: int = 0) -> dict:
    streams_of = jax.random.split(jax.random.key(seed), 10)
    return {
        "points": scatter_about(streams_of[0], (NODES, D), 1.0, 6.0, ((0, 128),)),
        "w_query": draw_w_query(jax.random.fold_in(streams_of[9], 71), 0),
        "w_key": scatter_about(streams_of[2], (D, D), D ** -0.5, 0.375),
        "w_value": scatter_about(streams_of[3], (D, D), D ** -0.5, 0.375),
        "w_out": scatter_about(streams_of[4], (D, D), D ** -0.5, 0.375),
        "gain": jnp.clip(1.0 + 0.15 * jax.random.normal(streams_of[5], (D,), jnp.float32), 0.25, 1.75),
        "cell_counts": draw_cell_counts(jax.random.fold_in(streams_of[9], 71), 0),
        "tile_slots": draw_tile_slots(jax.random.fold_in(streams_of[9], 71), 0),
        "edge_masks": place_ends((jax.random.randint(streams_of[8], (N_DST, N_SRC, TILES, TILE, TILE), 0, 64) < 1).astype(jnp.int32), jax.random.fold_in(streams_of[8], 1), 0, 1),
    }


def inverse_sinh(ratio):
    return jnp.log(ratio + jnp.sqrt(ratio * ratio + 1.0))

def log_map(points):
    values_f = points.astype(jnp.float32)
    radius = jnp.sqrt(lax.optimization_barrier(jnp.sum(values_f * values_f, axis=-1, keepdims=True)) + 1e-06)
    root_width = math.sqrt(points.shape[-1])
    return (root_width * inverse_sinh(radius / root_width) * values_f / radius).astype(jnp.bfloat16)

def exp_map(normed):
    radius = jnp.sqrt(lax.optimization_barrier(jnp.sum(normed * normed, axis=-1, keepdims=True)) + 1e-06)
    root_width = math.sqrt(normed.shape[-1])
    return (root_width * jnp.sinh(radius / root_width) * normed / radius).astype(jnp.bfloat16)

def project(rows, weight):
    return jnp.dot(rows, weight, preferred_element_type=jnp.float32).astype(jnp.bfloat16)

def reference(points, w_query, w_key, w_value, w_out, gain, cell_counts, tile_slots, edge_masks):
    head_size = D // HEADS
    score_scale = 1.0 / math.sqrt(head_size)
    tangent = log_map(points)
    queries = project(tangent, w_query)
    keys = project(tangent, w_key)
    values = project(tangent, w_value)
    block_rows = N_SRC * NODE_DEV
    row_tiles = block_rows // TILE
    col_tiles = N_DST * NODE_DEV // TILE
    key_src = keys.reshape(N_DST, N_SRC, NODE_DEV, D).transpose(1, 0, 2, 3).reshape(N_SRC, col_tiles, TILE, HEADS, head_size)
    value_src = values.reshape(N_DST, N_SRC, NODE_DEV, D).transpose(1, 0, 2, 3).reshape(N_SRC, col_tiles, TILE, HEADS, head_size)
    query_blocks = queries.reshape(N_DST, row_tiles, TILE, HEADS, head_size)
    key_blocks = keys.reshape(N_DST, block_rows, HEADS, head_size)
    value_blocks = values.reshape(N_DST, block_rows, HEADS, head_size)
    live_slots = jnp.arange(TILES, dtype=jnp.int32)[None, None, :] < cell_counts[:, :, None]
    src_ids = jnp.arange(N_SRC, dtype=jnp.int32)[:, None]
    inner_rows = jnp.arange(TILE, dtype=jnp.int32)

    def one_block(inputs):
        q_block, k_block, v_block, slot_grid, mask_grid, live_grid = inputs
        row_ids = (slot_grid // col_tiles).astype(jnp.int32)
        col_ids = (slot_grid % col_tiles).astype(jnp.int32)
        q_tiles = q_block[row_ids].astype(jnp.float32)
        k_tiles = key_src[src_ids, col_ids].astype(jnp.float32)
        v_tiles = value_src[src_ids, col_ids].astype(jnp.float32)
        scores = jnp.einsum('stihe,stjhe->sthij', q_tiles, k_tiles, precision=lax.Precision.HIGHEST) * score_scale
        edge_live = ((mask_grid == 1) & live_grid[:, :, None, None])[:, :, None]
        tile_max = lax.optimization_barrier(jnp.max(jnp.where(edge_live, scores, -jnp.inf), axis=-1))
        q_rows = q_block.reshape(block_rows, HEADS, head_size).astype(jnp.float32)
        self_score = jnp.einsum('rhe,rhe->hr', q_rows, k_block.astype(jnp.float32), precision=lax.Precision.HIGHEST) * score_scale
        flat_rows = (row_ids[:, :, None] * TILE + inner_rows[None, None, :]).reshape(-1)
        row_max = self_score.at[:, flat_rows].max(tile_max.transpose(2, 0, 1, 3).reshape(HEADS, -1))
        gathered_max = row_max[:, flat_rows].reshape(HEADS, N_SRC, TILES, TILE).transpose(1, 2, 0, 3)
        weights = jnp.where(edge_live, jnp.exp(scores - gathered_max[..., None]), 0.0)
        tile_sum = lax.optimization_barrier(jnp.sum(weights, axis=-1))
        self_exp = jnp.exp(self_score - row_max)
        row_sum = self_exp.at[:, flat_rows].add(tile_sum.transpose(2, 0, 1, 3).reshape(HEADS, -1))
        weights_low = lax.optimization_barrier(weights.astype(jnp.bfloat16)).astype(jnp.float32)
        tile_acc = jnp.einsum('sthij,stjhe->stihe', weights_low, v_tiles, precision=lax.Precision.HIGHEST)
        self_weight = lax.optimization_barrier(self_exp.astype(jnp.bfloat16)).astype(jnp.float32)
        row_acc = self_weight.T[:, :, None] * v_block.astype(jnp.float32)
        row_acc = row_acc.at[flat_rows].add(tile_acc.reshape(-1, HEADS, head_size))
        mixed_rows = row_acc / row_sum.T[:, :, None]
        return mixed_rows.reshape(block_rows, D).astype(jnp.bfloat16)
    mixed = lax.map(one_block, (query_blocks, key_blocks, value_blocks, tile_slots, edge_masks, live_slots))
    mixed = mixed.reshape(-1, D)
    shifted = tangent.astype(jnp.float32) + jnp.dot(mixed, w_out, preferred_element_type=jnp.float32)
    normed = shifted / jnp.sqrt(lax.optimization_barrier(jnp.mean(shifted * shifted, axis=-1, keepdims=True)) + 1e-06) * gain
    return exp_map(normed)
```

```python
import functools
import math

import jax
import jax.numpy as jnp
from jax import lax
from jax.experimental import pallas as pl
from jax.experimental.pallas import tpu as pltpu
from jax.sharding import PartitionSpec as P

HEADS = 4
TILE = 128
PAIR = 2 * TILE
VROWS = TILE + 16
MASKED = -1e30
FLOOR = -1e29
PREP = 8
F32 = jnp.float32
BF16 = jnp.bfloat16
VM = pltpu.VMEM
SM = pltpu.SMEM


def inverse_sinh(ratio):
    return jnp.log(ratio + jnp.sqrt(ratio * ratio + 1.0))


def log_map(points):
    values_f = points.astype(F32)
    radius = jnp.sqrt(jnp.sum(values_f * values_f, axis=-1, keepdims=True) + 1e-06)
    root_width = math.sqrt(points.shape[-1])
    return (root_width * inverse_sinh(radius / root_width) * values_f / radius).astype(BF16)


def gray(delta):
    return delta ^ (delta >> 1)


def prep_kernel(tiles, meta, slots, mask_ref, bias_ref, tile_out, spot_out, count_out):
    step = pl.program_id(0)
    me_dst, me_src, live = meta[0], meta[1], meta[2]

    @pl.when(step == 0)
    def _():
        for group in range(4):
            count_out[group] = 0

    for member in range(PREP):
        slot = step * PREP + member

        @pl.when(slot < live)
        def _():
            named = slots[slot]
            group = gray((named >> 5) ^ me_src)
            delta = (named & 31) ^ me_dst
            spot = (delta & 1) * 16 + gray((delta >> 3) & 3) * 4 + gray((delta >> 1) & 3)
            at = count_out[group]
            tile_out[group, at] = slot
            spot_out[group, at] = spot
            tile_out[group, at + 1] = tiles
            spot_out[group, at + 1] = 0
            count_out[group] = at + 1
            bias = jnp.where(mask_ref[member] == 1, 0.0, MASKED).astype(F32)
            bias_ref[member] = bias.T.astype(BF16)


def prepare(meta, slots, masks):
    tiles = masks.shape[0]
    return pl.pallas_call(
        functools.partial(prep_kernel, tiles),
        grid=(tiles // PREP,),
        in_specs=[
            pl.BlockSpec(memory_space=SM),
            pl.BlockSpec(memory_space=SM),
            pl.BlockSpec((PREP, TILE, TILE), lambda i: (i, 0, 0)),
        ],
        out_specs=[
            pl.BlockSpec((PREP, TILE, TILE), lambda i: (i, 0, 0)),
            pl.BlockSpec(memory_space=SM),
            pl.BlockSpec(memory_space=SM),
            pl.BlockSpec(memory_space=SM),
        ],
        out_shape=[
            jax.ShapeDtypeStruct((tiles, TILE, TILE), BF16),
            jax.ShapeDtypeStruct((4, 40), jnp.int32),
            jax.ShapeDtypeStruct((4, 40), jnp.int32),
            jax.ShapeDtypeStruct((4,), jnp.int32),
        ],
        cost_estimate=pl.CostEstimate(flops=1 << 20, bytes_accessed=6 << 20, transcendentals=0),
        name="prep",
    )(meta, slots, masks)


def nt_dot(left, right):
    return lax.dot_general(left, right, (((1,), (1,)), ((), ())), preferred_element_type=F32)


def attend_kernel(
    meta, tile_list, spot_list, counts, bias_hbm, near_ref, far_ref, block_ref, wq_ref, wk_ref, wv_ref,
    part_ref, bias_ref, key_ref, value_ref, query_ref, score_ref, acc_ref, sem,
):
    tiles = bias_hbm.shape[0]
    fetch = pltpu.make_async_copy(bias_hbm, bias_ref.at[pl.ds(0, tiles)], sem)
    fetch.start()
    bias_ref[tiles] = jnp.full((TILE, TILE), MASKED, BF16)
    for group in range(4):
        qt = nt_dot(wq_ref[...], block_ref[group]).astype(BF16) * jnp.asarray(0.125, BF16)
        zero = jnp.zeros((64, TILE), BF16)
        for half in range(2):
            upper = jnp.concatenate([qt[half * TILE : half * TILE + 64], zero], axis=1)
            lower = jnp.concatenate([zero, qt[half * TILE + 64 : half * TILE + TILE]], axis=1)
            query_ref[group, half] = jnp.concatenate([upper, lower], axis=0)

    wk = wk_ref[...]
    wv = wv_ref[...]
    ones = jnp.ones((VROWS - TILE, TILE), BF16)
    for side, rows_ref in ((0, near_ref), (1, far_ref)):

        @pl.loop(0, 4)
        def _(step):
            for member in range(4):
                spot = step * 4 + member
                rows = rows_ref[pl.ds(pl.multiple_of(spot * TILE, TILE), TILE), :]
                at = side * 16 + spot
                key_ref[at] = jnp.dot(rows, wk, preferred_element_type=F32).astype(BF16)
                vt = nt_dot(wv, rows).astype(BF16)
                for half in range(2):
                    value_ref[at, half, pl.ds(0, TILE), :] = vt[half * TILE : (half + 1) * TILE]
                    value_ref[at, half, pl.ds(TILE, VROWS - TILE), :] = ones

    fetch.wait()
    for group in range(4):
        count = counts[group]
        trips = (count + 1) // 2
        target = gray_inverse_of(group, meta[1])

        def score_step(trip, tops):
            new = list(tops)
            for member in range(2):
                at = trip * 2 + member
                tile = tile_list[group, at]
                spot = spot_list[group, at]
                bias = bias_ref[tile].astype(F32)
                bias = jnp.concatenate([bias, bias], axis=1)
                for half in range(2):
                    keys = key_ref[spot, :, half * TILE : (half + 1) * TILE]
                    score = jnp.dot(keys, query_ref[group, half], preferred_element_type=F32) + bias
                    score_ref[at, half] = score
                    new[half] = jnp.maximum(new[half], jnp.max(score.reshape(16, 8, PAIR), axis=0))
            return tuple(new)

        start = jnp.full((8, PAIR), FLOOR, F32)
        tops = lax.fori_loop(0, trips, score_step, (start, start))
        tops = [jnp.max(top, axis=0, keepdims=True) for top in tops]
        acc_ref[...] = jnp.zeros_like(acc_ref)

        def mix_step(trip, _):
            at = trip * 2
            first, second = spot_list[group, at], spot_list[group, at + 1]
            for half in range(2):
                low = jnp.exp(score_ref[at, half] - tops[half]).astype(BF16)
                high = jnp.exp(score_ref[at + 1, half] - tops[half]).astype(BF16)
                weights = jnp.concatenate([low, high], axis=0)
                values = jnp.concatenate([value_ref[first, half], value_ref[second, half]], axis=1)
                acc_ref[half] += jnp.dot(values, weights, preferred_element_type=F32)
            return 0

        lax.fori_loop(0, trips, mix_step, 0)
        for half in range(2):
            acc = acc_ref[half]
            part_ref[target, pl.ds(half * TILE, 64), :] = acc[:64, :TILE]
            part_ref[target, pl.ds(half * TILE + 64, 64), :] = acc[64:TILE, TILE:]
            for side in range(2):
                lanes = slice(side * TILE, (side + 1) * TILE)
                row = 256 + half * 2 + side
                part_ref[target, pl.ds(row, 1), :] = tops[half][:, lanes]
                part_ref[target, pl.ds(row + 4, 1), :] = acc[TILE : TILE + 1, lanes]


def gray_inverse_of(group, me_src):
    return (group ^ (group >> 1)) ^ me_src


def attend(meta, tile_list, spot_list, counts, bias, near, far, block, wq_t, w_key, wv_t):
    tiles = bias.shape[0]
    vm = pl.BlockSpec(memory_space=VM)
    sm = pl.BlockSpec(memory_space=SM)
    return pl.pallas_call(
        attend_kernel,
        in_specs=[sm, sm, sm, sm, pl.BlockSpec(memory_space=pl.ANY)] + [vm] * 6,
        out_specs=vm,
        out_shape=jax.ShapeDtypeStruct((4, 264, TILE), F32),
        scratch_shapes=[
            VM((tiles + 1, TILE, TILE), BF16),
            VM((32, TILE, 256), BF16),
            VM((32, 2, VROWS, TILE), BF16),
            VM((4, 2, TILE, PAIR), BF16),
            VM((34, 2, TILE, PAIR), F32),
            VM((2, VROWS, PAIR), F32),
            pltpu.SemaphoreType.DMA,
        ],
        compiler_params=pltpu.CompilerParams(vmem_limit_bytes=48 << 20),
        cost_estimate=pl.CostEstimate(flops=4 << 30, bytes_accessed=8 << 20, transcendentals=4 << 20),
        name="attend",
    )(meta, tile_list, spot_list, counts, bias, near, far, block, wq_t, w_key, wv_t)


def finish_kernel(part_ref, tangent_ref, wq_ref, wk_ref, wv_ref, wo_ref, gain_ref, out_ref):
    tangent = tangent_ref[...]
    qt = nt_dot(wq_ref[...], tangent).astype(BF16).astype(F32)
    kt = nt_dot(wk_ref[...], tangent).astype(BF16).astype(F32)
    vt = nt_dot(wv_ref[...], tangent).astype(BF16).astype(F32)
    product = qt * kt * 0.125
    mixed = []
    for head in range(HEADS):
        rows = slice(head * 64, head * 64 + 64)
        own = jnp.sum(product[rows], axis=0, keepdims=True)
        tops = [part_ref[cell, pl.ds(256 + head, 1), :] for cell in range(4)]
        top = own
        for other in tops:
            top = jnp.maximum(top, other)
        own_exp = jnp.exp(own - top)
        total = own_exp
        weighted = own_exp.astype(BF16).astype(F32) * vt[rows]
        for cell in range(4):
            factor = jnp.exp(tops[cell] - top)
            total += part_ref[cell, pl.ds(260 + head, 1), :] * factor
            weighted += part_ref[cell, pl.ds(head * 64, 64), :] * factor
        mixed.append((weighted / total).astype(BF16))
    mixed = jnp.concatenate(mixed, axis=0)
    shifted = tangent.astype(F32) + lax.dot_general(
        mixed, wo_ref[...], (((0,), (0,)), ((), ())), preferred_element_type=F32
    )
    normed = shifted / jnp.sqrt(jnp.mean(shifted * shifted, axis=-1, keepdims=True) + 1e-06) * gain_ref[...]
    radius = jnp.sqrt(jnp.sum(normed * normed, axis=-1, keepdims=True) + 1e-06)
    ratio = radius / 16.0
    square = ratio * ratio
    series = ratio * (
        1.0 + square / 6.0 * (1.0 + square / 20.0 * (1.0 + square / 42.0 * (1.0 + square / 72.0)))
    )
    plain = 0.5 * (jnp.exp(ratio) - jnp.exp(-ratio))
    stretched = jnp.where(ratio < 0.75, series, plain)
    out_ref[...] = (16.0 * stretched * normed / radius).astype(BF16)


def finish(part, tangent, wq_t, wk_t, wv_t, w_out, gain):
    vm = pl.BlockSpec(memory_space=VM)
    return pl.pallas_call(
        finish_kernel,
        in_specs=[vm] * 7,
        out_specs=vm,
        out_shape=jax.ShapeDtypeStruct(tangent.shape, BF16),
        cost_estimate=pl.CostEstimate(flops=1 << 26, bytes_accessed=1 << 20, transcendentals=1 << 12),
        name="finish",
    )(part, tangent, wq_t, wk_t, wv_t, w_out, gain)


def swap(value, axis, size, mask):
    return lax.ppermute(value, axis, [(at, at ^ mask) for at in range(size)])


def grow(value, axis, size, mask):
    return jnp.concatenate([value, swap(value, axis, size, mask)], axis=0)


def per_device(points, w_query, w_key, w_value, w_out, gain, cell_counts, tile_slots, edge_masks):
    me_dst = lax.axis_index("dst")
    me_src = lax.axis_index("src")
    meta = jnp.stack([me_dst, me_src, cell_counts[0, 0]]).astype(jnp.int32)
    tangent = log_map(points)
    near = tangent
    block = tangent
    for mask in (1, 3):
        block = grow(block, "src", 4, mask)
    for mask in (2, 6, 8, 24):
        near = grow(near, "dst", 32, mask)
    far = swap(near, "dst", 32, 1)
    bias, tile_list, spot_list, counts = prepare(meta, tile_slots[0, 0], edge_masks[0, 0])
    wq_t, wk_t, wv_t = w_query.T, w_key.T, w_value.T
    block = block.reshape(4, TILE, 256)
    part = attend(meta, tile_list, spot_list, counts, bias, near, far, block, wq_t, w_key, wv_t)
    part = lax.all_to_all(part, "src", 0, 0)
    return finish(part, tangent, wq_t, wk_t, wv_t, w_out, gain[None, :])


def solution(mesh):
    return jax.shard_map(
        per_device,
        mesh=mesh,
        in_specs=(
            P(("dst", "src"), None),
            P(),
            P(),
            P(),
            P(),
            P(),
            P("dst", "src"),
            P("dst", "src", None),
            P("dst", "src", None, None, None),
        ),
        out_specs=P(("dst", "src"), None),
        check_vma=False,
    )
```

```python
import math

import jax
import jax.numpy as jnp
from jax import lax
from jax.experimental import pallas as pl
from jax.experimental.pallas import tpu as pltpu
from jax.sharding import PartitionSpec as P


HEADS = 4
TILE = 128
PAIR = 2 * TILE
VROWS = TILE + 16
MASKED = -1e30
FLOOR = -1e29
PREP = 8
GROUP = 8
UNROLL = 4
F32 = jnp.float32
BF16 = jnp.bfloat16
VM = pltpu.VMEM
SM = pltpu.SMEM


def inverse_sinh(ratio):
    return jnp.log(ratio + jnp.sqrt(ratio * ratio + 1.0))


def log_map(points):
    values_f = points.astype(F32)
    radius = jnp.sqrt(jnp.sum(values_f * values_f, axis=-1, keepdims=True) + 1e-06)
    root_width = math.sqrt(points.shape[-1])
    return (root_width * inverse_sinh(radius / root_width) * values_f / radius).astype(BF16)


def gray(delta):
    return delta ^ (delta >> 1)


def prep_kernel(meta, slots, mask_ref, bias_ref, spot_out, group_out, pair_out, count_out, open_ref):
    step = pl.program_id(0)
    me_dst, me_src, live = meta[0], meta[1], meta[2]
    spare = slots.shape[0]
    trash = spare // 2 + 4 + UNROLL

    @pl.when(step == 0)
    def _():
        count_out[0] = 0
        for group in range(4):
            open_ref[group] = -1
        spot_out[spare] = 0

    opened = [open_ref[group] for group in range(4)]
    count = count_out[0]
    for member in range(PREP):
        slot = step * PREP + member
        named = slots[slot]
        group = gray((named >> 5) ^ me_src)
        delta = (named & 31) ^ me_dst
        spot_out[slot] = (delta & 1) * 16 + gray((delta >> 3) & 3) * 4 + gray((delta >> 1) & 3)
        group_out[slot] = group
        is_live = slot < live
        was_open = opened[3]
        for other in range(3):
            was_open = jnp.where(group == other, opened[other], was_open)
        is_fresh = was_open < 0
        fresh = is_fresh.astype(jnp.int32)
        pair = jnp.where(is_live, jnp.where(is_fresh, count, was_open), trash)
        count = count + jnp.where(is_live, fresh, 0)
        after = jnp.where(is_fresh, pair, -1)
        for other in range(4):
            opened[other] = jnp.where(is_live & (group == other), after, opened[other])
        pair_out[pair * 2 + 1] = spare
        pair_out[pair * 2 + 1 - fresh] = slot
        wanted = jnp.where(is_live, 1, 2)
        bias_ref[member] = jnp.where(mask_ref[member] == wanted, 0.0, MASKED).astype(BF16)
    count_out[0] = count
    for group in range(4):
        open_ref[group] = opened[group]

    @pl.when(step == pl.num_programs(0) - 1)
    def _():
        count = count_out[0]
        for extra in range(2 * UNROLL):
            pair_out[count * 2 + extra] = spare
        group_out[spare] = 0


def prepare(meta, slots, masks):
    tiles = masks.shape[0]
    sm = pl.BlockSpec(memory_space=SM)
    return pl.pallas_call(
        prep_kernel,
        grid=(tiles // PREP,),
        in_specs=[sm, sm, pl.BlockSpec((PREP, TILE, TILE), lambda i: (i, 0, 0))],
        out_specs=[pl.BlockSpec((PREP, TILE, TILE), lambda i: (i, 0, 0)), sm, sm, sm, sm],
        out_shape=[
            jax.ShapeDtypeStruct((tiles, TILE, TILE), BF16),
            jax.ShapeDtypeStruct((tiles + 8,), jnp.int32),
            jax.ShapeDtypeStruct((tiles + 8,), jnp.int32),
            jax.ShapeDtypeStruct((tiles + 10 + 2 * UNROLL,), jnp.int32),
            jax.ShapeDtypeStruct((1,), jnp.int32),
        ],
        scratch_shapes=[SM((4,), jnp.int32)],
        compiler_params=pltpu.CompilerParams(vmem_limit_bytes=8 << 20),
        cost_estimate=pl.CostEstimate(flops=1 << 20, bytes_accessed=6 << 20, transcendentals=0),
        name="prep",
    )(meta, slots, masks)


def nt_dot(left, right):
    return lax.dot_general(left, right, (((1,), (1,)), ((), ())), preferred_element_type=F32)


def project_rows(first_ref, second_ref, wk, wv, key_ref, value_ref, base):
    ones = jnp.ones((VROWS - TILE, TILE), BF16)

    @pl.loop(0, 4)
    def _(step):
        rows = []
        for member in range(4):
            rows.append(first_ref[pl.ds(pl.multiple_of((step * 4 + member) * 64, 64), 64), :])
            rows.append(second_ref[pl.ds(pl.multiple_of((member * 4 + step) * 64, 64), 64), :])
        rows = jnp.concatenate(rows, axis=0)
        keys = jnp.dot(rows, wk, preferred_element_type=F32).astype(BF16)
        values = nt_dot(wv, rows).astype(BF16)
        for member in range(4):
            at = base + step * 4 + member
            span = slice(member * TILE, (member + 1) * TILE)
            key_ref[at] = keys[span]
            for half in range(2):
                value_ref[at, half, pl.ds(0, TILE), :] = values[half * TILE : (half + 1) * TILE, span]
                value_ref[at, half, pl.ds(TILE, VROWS - TILE), :] = ones


def project_kernel(
    first_ref, second_ref, block_ref, wq_ref, wk_ref, wv_ref, key_ref, value_ref, query_ref, turned_ref, own_ref, self_ref
):
    wq, wk = wq_ref[...], wk_ref[...]
    wv_t = wv_ref[...].astype(F32).T.astype(BF16)
    turned_ref[...] = wv_t
    lane = lax.broadcasted_iota(jnp.int32, (TILE, TILE), 1)
    for group in range(4):
        rows = jnp.dot(block_ref[group], wq, preferred_element_type=F32).astype(BF16).astype(F32) * 0.125
        for half in range(2):
            part = rows[:, half * TILE : (half + 1) * TILE]
            query_ref[group, half, pl.ds(0, TILE), :] = jnp.where(lane < 64, part, 0.0).astype(BF16)
            query_ref[group, half, pl.ds(TILE, TILE), :] = jnp.where(lane < 64, 0.0, part).astype(BF16)
        if group == 0:
            own_keys = jnp.dot(block_ref[0], wk, preferred_element_type=F32).astype(BF16).astype(F32)
            product = (rows * own_keys).T
            for head in range(HEADS):
                total = jnp.sum(product[head * 64 : (head + 1) * 64], axis=0, keepdims=True)
                self_ref[pl.ds(head, 1), :] = total
            own_ref[...] = nt_dot(wv_t, block_ref[0]).astype(BF16)
    project_rows(first_ref, second_ref, wk, wv_t, key_ref, value_ref, 0)


def project(first, second, block, w_query, w_key, w_value):
    vm = pl.BlockSpec(memory_space=VM)
    return pl.pallas_call(
        project_kernel,
        in_specs=[vm] * 6,
        out_specs=[vm] * 6,
        out_shape=[
            jax.ShapeDtypeStruct((16, TILE, 256), BF16),
            jax.ShapeDtypeStruct((16, 2, VROWS, TILE), BF16),
            jax.ShapeDtypeStruct((4, 2, PAIR, TILE), BF16),
            jax.ShapeDtypeStruct((256, 256), BF16),
            jax.ShapeDtypeStruct((256, TILE), BF16),
            jax.ShapeDtypeStruct((HEADS, TILE), F32),
        ],
        compiler_params=pltpu.CompilerParams(vmem_limit_bytes=8 << 20),
        cost_estimate=pl.CostEstimate(flops=1 << 29, bytes_accessed=4 << 20, transcendentals=0),
        name="project",
    )(first, second, block, w_query, w_key, w_value)


def attend_kernel(
    meta, spot_list, group_list, pair_list, counts, bias_hbm, key_hbm, value_hbm, query_ref, first_ref, second_ref,
    wk_ref, wv_ref, part_ref, bias_ref, key_ref, value_ref, top_ref, acc_ref, score_ref, sem,
):
    tiles = bias_hbm.shape[0]
    copies = [
        pltpu.make_async_copy(bias_hbm, bias_ref, sem.at[0]),
        pltpu.make_async_copy(key_hbm, key_ref.at[pl.ds(0, 16)], sem.at[1]),
        pltpu.make_async_copy(value_hbm, value_ref.at[pl.ds(0, 16)], sem.at[2]),
    ]
    for copy in copies:
        copy.start()
    score_ref[tiles] = jnp.full((2, TILE, PAIR), MASKED, F32)
    top_ref[...] = jnp.full(top_ref.shape, FLOOR, F32)
    acc_ref[...] = jnp.zeros(acc_ref.shape, F32)
    project_rows(first_ref, second_ref, wk_ref[...], wv_ref[...], key_ref, value_ref, 16)
    for copy in copies:
        copy.wait()
    row = lax.broadcasted_iota(jnp.int32, (TILE, TILE), 0)
    lane = lax.broadcasted_iota(jnp.int32, (TILE, TILE), 1)
    eye = jnp.where(row == lane, 1.0, 0.0).astype(BF16)

    def score_step(trip, _):
        for member in range(GROUP):
            tile = trip * GROUP + member
            spot = spot_list[tile]
            group = group_list[tile]
            bias = bias_ref[tile]
            bias = jnp.concatenate([bias, bias], axis=0)
            for half in range(2):
                keys = jnp.concatenate([key_ref[spot, :, half * TILE : (half + 1) * TILE], eye], axis=1)
                queries = jnp.concatenate([query_ref[group, half], bias], axis=1)
                scores = nt_dot(keys, queries)
                score_ref[tile, half] = scores
                top = jnp.max(scores.reshape(16, 8, PAIR), axis=0)
                top_ref[group, half] = jnp.maximum(top_ref[group, half], top)
        return 0

    lax.fori_loop(0, (meta[2] + GROUP - 1) // GROUP, score_step, 0)
    for group in range(4):
        for half in range(2):
            top = jnp.max(top_ref[group, half], axis=0, keepdims=True)
            top_ref[group, half] = jnp.broadcast_to(top, (8, PAIR))

    def mix_step(trip, _):
        for member in range(UNROLL):
            pair = trip * UNROLL + member
            first, second = pair_list[pair * 2], pair_list[pair * 2 + 1]
            group = group_list[first]
            near, far = spot_list[first], spot_list[second]
            for half in range(2):
                top = top_ref[group, half, pl.ds(0, 1), :]
                weights = jnp.concatenate(
                    [jnp.exp(score_ref[tile, half] - top).astype(BF16) for tile in (first, second)], axis=0
                )
                values = jnp.concatenate([value_ref[near, half], value_ref[far, half]], axis=1)
                acc_ref[group, half] += jnp.dot(values, weights, preferred_element_type=F32)
        return 0

    lax.fori_loop(0, (counts[0] + UNROLL - 1) // UNROLL, mix_step, 0)
    for group in range(4):
        target = gray(group) ^ meta[1]
        for half in range(2):
            acc = acc_ref[group, half]
            part_ref[target, pl.ds(half * TILE, 64), :] = acc[:64, :TILE].astype(BF16)
            part_ref[target, pl.ds(half * TILE + 64, 64), :] = acc[64:TILE, TILE:].astype(BF16)
        rows = []
        for head in range(HEADS):
            half, lanes = head // 2, slice((head % 2) * TILE, (head % 2 + 1) * TILE)
            rows.append(top_ref[group, half, pl.ds(0, 1), lanes])
        for head in range(HEADS):
            half, lanes = head // 2, slice((head % 2) * TILE, (head % 2 + 1) * TILE)
            rows.append(acc_ref[group, half, pl.ds(TILE, 1), lanes])
        rest = jnp.concatenate(rows, axis=0)
        pieces = []
        for _ in range(4):
            piece = rest.astype(BF16)
            pieces.append(piece)
            rest = rest - piece.astype(F32)
        part_ref[target, pl.ds(256, 32), :] = jnp.concatenate(pieces, axis=0)


def attend(meta, lists, bias, keys, values, queries, first, second, w_key, wv_t):
    tiles = bias.shape[0]
    vm = pl.BlockSpec(memory_space=VM)
    sm = pl.BlockSpec(memory_space=SM)
    anywhere = pl.BlockSpec(memory_space=pl.ANY)
    return pl.pallas_call(
        attend_kernel,
        in_specs=[sm] * 5 + [anywhere] * 3 + [vm] * 5,
        out_specs=vm,
        out_shape=jax.ShapeDtypeStruct((4, 288, TILE), BF16),
        scratch_shapes=[
            VM((tiles, TILE, TILE), BF16),
            VM((32, TILE, 256), BF16),
            VM((32, 2, VROWS, TILE), BF16),
            VM((4, 2, 8, PAIR), F32),
            VM((4, 2, VROWS, PAIR), F32),
            VM((tiles + 1, 2, TILE, PAIR), F32),
            pltpu.SemaphoreType.DMA((3,)),
        ],
        compiler_params=pltpu.CompilerParams(vmem_limit_bytes=34 << 20),
        cost_estimate=pl.CostEstimate(flops=4 << 30, bytes_accessed=8 << 20, transcendentals=4 << 20),
        name="attend",
    )(meta, *lists, bias, keys, values, queries, first, second, w_key, wv_t)


def finish_kernel(part_ref, tangent_ref, own_ref, self_ref, wo_ref, gain_ref, out_ref):
    tangent = tangent_ref[...]
    vt = own_ref[...].astype(F32)
    stats = []
    for cell in range(4):
        pieces = part_ref[cell, pl.ds(256, 32), :].astype(F32)
        stats.append(pieces[:8] + pieces[8:16] + pieces[16:24] + pieces[24:])
    mixed = []
    for head in range(HEADS):
        rows = slice(head * 64, head * 64 + 64)
        own = self_ref[pl.ds(head, 1), :]
        tops = [stat[head : head + 1] for stat in stats]
        top = own
        for other in tops:
            top = jnp.maximum(top, other)
        own_exp = jnp.exp(own - top)
        total = own_exp
        weighted = own_exp.astype(BF16).astype(F32) * vt[rows]
        for cell in range(4):
            factor = jnp.exp(tops[cell] - top)
            total += stats[cell][4 + head : 5 + head] * factor
            weighted += part_ref[cell, pl.ds(head * 64, 64), :].astype(F32) * factor
        mixed.append((weighted / total).astype(BF16))
    mixed = jnp.concatenate(mixed, axis=0)
    shifted = tangent.astype(F32) + lax.dot_general(
        mixed, wo_ref[...], (((0,), (0,)), ((), ())), preferred_element_type=F32
    )
    normed = shifted / jnp.sqrt(jnp.mean(shifted * shifted, axis=-1, keepdims=True) + 1e-06) * gain_ref[...]
    radius = jnp.sqrt(jnp.sum(normed * normed, axis=-1, keepdims=True) + 1e-06)
    ratio = radius / 16.0
    square = ratio * ratio
    series = ratio * (
        1.0 + square / 6.0 * (1.0 + square / 20.0 * (1.0 + square / 42.0 * (1.0 + square / 72.0)))
    )
    plain = 0.5 * (jnp.exp(ratio) - jnp.exp(-ratio))
    stretched = jnp.where(ratio < 0.75, series, plain)
    out_ref[...] = (16.0 * stretched * normed / radius).astype(BF16)


def finish(part, tangent, own, self_score, w_out, gain):
    vm = pl.BlockSpec(memory_space=VM)
    return pl.pallas_call(
        finish_kernel,
        in_specs=[vm] * 6,
        out_specs=vm,
        out_shape=jax.ShapeDtypeStruct(tangent.shape, BF16),
        compiler_params=pltpu.CompilerParams(vmem_limit_bytes=8 << 20),
        cost_estimate=pl.CostEstimate(flops=1 << 26, bytes_accessed=1 << 20, transcendentals=1 << 12),
        name="finish",
    )(part, tangent, own, self_score, w_out, gain)


def swap(value, axis, size, mask):
    return lax.ppermute(value, axis, [(at, at ^ mask) for at in range(size)])


def grow(value, axis, size, mask):
    return jnp.concatenate([value, swap(value, axis, size, mask)], axis=0)


def per_device(points, w_query, w_key, w_value, w_out, gain, cell_counts, tile_slots, edge_masks):
    me_dst = lax.axis_index("dst")
    me_src = lax.axis_index("src")
    meta = jnp.stack([me_dst, me_src, cell_counts[0, 0]]).astype(jnp.int32)
    tangent = log_map(points)
    first, second, block = tangent[:64], tangent[64:], tangent
    for hop, (one, other) in enumerate(((2, 8), (6, 24), (8, 2), (24, 6))):
        new_first = grow(first, "dst", 32, one)
        second = grow(second, "dst", 32, other)
        first = new_first
        if hop < 2:
            block = grow(block, "src", 4, (1, 3)[hop])
            first, second, block = lax.optimization_barrier((first, second, block))
    far_first = swap(first, "dst", 32, 1)
    far_second = swap(second, "dst", 32, 1)
    bias, *lists = prepare(meta, tile_slots[0, 0], edge_masks[0, 0])
    keys, values, queries, wv_t, own, self_score = project(
        first, second, block.reshape(4, TILE, 256), w_query, w_key, w_value
    )
    part = attend(meta, lists, bias, keys, values, queries, far_first, far_second, w_key, wv_t)
    part = lax.all_to_all(part, "src", 0, 0)
    return finish(part, tangent, own, self_score, w_out, gain[None, :])


def solution(mesh):
    return jax.shard_map(
        per_device,
        mesh=mesh,
        in_specs=(
            P(("dst", "src"), None),
            P(),
            P(),
            P(),
            P(),
            P(),
            P("dst", "src"),
            P("dst", "src", None),
            P("dst", "src", None, None, None),
        ),
        out_specs=P(("dst", "src"), None),
        check_vma=False,
    )
```

```python
import functools
import math

import jax
import jax.numpy as jnp
from jax import lax
from jax.experimental import pallas as pl
from jax.experimental.pallas import tpu as pltpu
from jax.sharding import PartitionSpec as P


HEADS = 4
TILE = 128
PAIR = 2 * TILE
VROWS = TILE + 16
MASKED = -1e30
FLOOR = -1e29
PREP = 8
QUAD = 4
STRIDE = 40
F32 = jnp.float32
BF16 = jnp.bfloat16
VM = pltpu.VMEM
SM = pltpu.SMEM


def inverse_sinh(ratio):
    return jnp.log(ratio + jnp.sqrt(ratio * ratio + 1.0))


def log_map(points):
    values_f = points.astype(F32)
    radius = jnp.sqrt(jnp.sum(values_f * values_f, axis=-1, keepdims=True) + 1e-06)
    root_width = math.sqrt(points.shape[-1])
    return (root_width * inverse_sinh(radius / root_width) * values_f / radius).astype(BF16)


def gray(delta):
    return delta ^ (delta >> 1)


def prep_kernel(meta, slots, mask_hbm, bias_ref, spot_out, tile_out, count_out, mask_ref, sem):
    me_dst, me_src, live = meta[0], meta[1], meta[2]
    spare = slots.shape[0]

    def fetch(trip):
        span = pl.ds(trip * PREP, PREP)
        return pltpu.make_async_copy(mask_hbm.at[span], mask_ref.at[span], sem.at[trip])

    for trip in range(spare // PREP):
        fetch(trip).start()
    row = lax.broadcasted_iota(jnp.int32, (TILE, TILE), 0)
    lane = lax.broadcasted_iota(jnp.int32, (TILE, TILE), 1)
    eye = jnp.where(row == lane, 1.0, 0.0).astype(BF16)
    bias_ref[spare] = jnp.full((TILE, TILE), MASKED, BF16)
    spot_out[spare] = 0

    def step(trip, counts):
        counts = list(counts)
        fetch(trip).wait()
        for member in range(PREP):
            slot = trip * PREP + member
            named = slots[slot]
            group = gray((named >> 5) ^ me_src)
            delta = (named & 31) ^ me_dst
            spot_out[slot] = (delta & 1) * 16 + gray((delta >> 3) & 3) * 4 + gray((delta >> 1) & 3)
            at = counts[3]
            for other in range(3):
                at = jnp.where(group == other, counts[other], at)
            is_live = slot < live
            tile_out[jnp.where(is_live, group * STRIDE + at, 4 * STRIDE)] = slot
            for other in range(4):
                counts[other] = counts[other] + (is_live & (group == other)).astype(jnp.int32)
            wanted = jnp.where(is_live, 1, 2)
            bias = jnp.where(mask_ref[slot] == wanted, 0.0, MASKED).astype(BF16)
            bias_ref[slot] = nt_dot(eye, bias).astype(BF16)
        return tuple(counts)

    zero = jnp.int32(0)
    counts = lax.fori_loop(0, spare // PREP, step, (zero,) * 4)
    for group in range(4):
        count_out[group] = counts[group]
        for extra in range(QUAD):
            tile_out[group * STRIDE + counts[group] + extra] = spare


def prepare(meta, slots, masks):
    tiles = masks.shape[0]
    vm = pl.BlockSpec(memory_space=VM)
    sm = pl.BlockSpec(memory_space=SM)
    return pl.pallas_call(
        prep_kernel,
        in_specs=[sm, sm, pl.BlockSpec(memory_space=pltpu.HBM)],
        out_specs=[vm, sm, sm, sm],
        out_shape=[
            jax.ShapeDtypeStruct((tiles + 1, TILE, TILE), BF16),
            jax.ShapeDtypeStruct((tiles + 8,), jnp.int32),
            jax.ShapeDtypeStruct((4 * STRIDE + 8,), jnp.int32),
            jax.ShapeDtypeStruct((4,), jnp.int32),
        ],
        scratch_shapes=[VM(masks.shape, jnp.int32), pltpu.SemaphoreType.DMA((tiles // PREP,))],
        compiler_params=pltpu.CompilerParams(vmem_limit_bytes=8 << 20),
        cost_estimate=pl.CostEstimate(flops=1 << 20, bytes_accessed=6 << 20, transcendentals=0),
        name="prep",
    )(meta, slots, masks)


def nt_dot(left, right):
    return lax.dot_general(left, right, (((1,), (1,)), ((), ())), preferred_element_type=F32)


def project_rows(first_ref, second_ref, wk, wv, key_ref, value_ref, base):
    ones = jnp.ones((VROWS - TILE, TILE), BF16)

    @pl.loop(0, 4)
    def _(step):
        rows = []
        for member in range(4):
            rows.append(first_ref[pl.ds(pl.multiple_of((step * 4 + member) * 64, 64), 64), :])
            rows.append(second_ref[pl.ds(pl.multiple_of((member * 4 + step) * 64, 64), 64), :])
        rows = jnp.concatenate(rows, axis=0)
        keys = jnp.dot(rows, wk, preferred_element_type=F32).astype(BF16)
        values = nt_dot(wv, rows).astype(BF16)
        for member in range(4):
            at = base + step * 4 + member
            span = slice(member * TILE, (member + 1) * TILE)
            key_ref[at] = keys[span]
            for half in range(2):
                value_ref[at, half, pl.ds(0, TILE), :] = values[half * TILE : (half + 1) * TILE, span]
                value_ref[at, half, pl.ds(TILE, VROWS - TILE), :] = ones


def project_kernel(
    first_ref, second_ref, block_ref, wq_ref, wk_ref, wv_ref, key_ref, value_ref, query_ref, turned_ref, own_ref, self_ref
):
    wq, wk = wq_ref[...], wk_ref[...]
    wv_t = wv_ref[...].astype(F32).T.astype(BF16)
    turned_ref[...] = wv_t
    wq_t = wq.astype(F32).T.astype(BF16)
    zero = jnp.zeros((64, TILE), BF16)
    for group in range(4):
        qt = nt_dot(wq_t, block_ref[group]).astype(BF16).astype(F32) * 0.125
        low = qt.astype(BF16)
        for half in range(2):
            upper = jnp.concatenate([low[half * TILE : half * TILE + 64], zero], axis=1)
            lower = jnp.concatenate([zero, low[half * TILE + 64 : half * TILE + TILE]], axis=1)
            query_ref[group, half] = jnp.concatenate([upper, lower], axis=0)
        if group == 0:
            wk_t = wk.astype(F32).T.astype(BF16)
            product = qt * nt_dot(wk_t, block_ref[0]).astype(BF16).astype(F32)
            for head in range(HEADS):
                total = jnp.sum(product[head * 64 : (head + 1) * 64], axis=0, keepdims=True)
                self_ref[pl.ds(head, 1), :] = total
            own_ref[...] = nt_dot(wv_t, block_ref[0]).astype(BF16)
    project_rows(first_ref, second_ref, wk, wv_t, key_ref, value_ref, 0)


def project(first, second, block, w_query, w_key, w_value):
    vm = pl.BlockSpec(memory_space=VM)
    return pl.pallas_call(
        project_kernel,
        in_specs=[vm] * 6,
        out_specs=[vm] * 6,
        out_shape=[
            jax.ShapeDtypeStruct((16, TILE, 256), BF16),
            jax.ShapeDtypeStruct((16, 2, VROWS, TILE), BF16),
            jax.ShapeDtypeStruct((4, 2, TILE, PAIR), BF16),
            jax.ShapeDtypeStruct((256, 256), BF16),
            jax.ShapeDtypeStruct((256, TILE), BF16),
            jax.ShapeDtypeStruct((HEADS, TILE), F32),
        ],
        compiler_params=pltpu.CompilerParams(vmem_limit_bytes=8 << 20),
        cost_estimate=pl.CostEstimate(flops=1 << 29, bytes_accessed=4 << 20, transcendentals=0),
        name="project",
    )(first, second, block, w_query, w_key, w_value)


def attend_rows(
    group, spot_list, tile_list, counts, bias_ref, query_ref, key_ref, value_ref, part_ref, acc_ref, score_ref
):
    base = group * STRIDE
    count = counts[group]
    quads = (count + 1) // QUAD
    rest = (count - quads * QUAD + 1) // 2

    def score(start, size, tops):
        tops = list(tops)
        names = [tile_list[base + start + member] for member in range(size)]
        spots = [spot_list[name] for name in names]
        for half in range(2):
            keys = jnp.concatenate([key_ref[spot, :, half * TILE : (half + 1) * TILE] for spot in spots], axis=0)
            scores = jnp.dot(keys, query_ref[group, half], preferred_element_type=F32)
            for member in range(size):
                bias = bias_ref[names[member]].astype(F32)
                part = scores[member * TILE : (member + 1) * TILE] + jnp.concatenate([bias, bias], axis=1)
                score_ref[start + member, half] = part
                tops[half] = jnp.maximum(tops[half], jnp.max(part.reshape(16, 8, PAIR), axis=0))
        return tuple(tops)

    floor = jnp.full((8, PAIR), FLOOR, F32)
    tops = lax.fori_loop(0, quads, lambda trip, tops: score(trip * QUAD, QUAD, tops), (floor, floor))
    tops = lax.fori_loop(0, rest, lambda trip, tops: score(quads * QUAD + trip * 2, 2, tops), tops)
    tops = [jnp.max(top, axis=0, keepdims=True) for top in tops]
    acc_ref[...] = jnp.zeros(acc_ref.shape, F32)

    def mix(start, size):
        spots = [spot_list[tile_list[base + start + member]] for member in range(size)]
        for half in range(2):
            weights = [jnp.exp(score_ref[start + member, half] - tops[half]).astype(BF16) for member in range(size)]
            values = jnp.concatenate([value_ref[spot, half] for spot in spots], axis=1)
            acc_ref[half] += jnp.dot(values, jnp.concatenate(weights, axis=0), preferred_element_type=F32)
        return 0

    lax.fori_loop(0, quads, lambda trip, _: mix(trip * QUAD, QUAD), 0)
    lax.fori_loop(0, rest, lambda trip, _: mix(quads * QUAD + trip * 2, 2), 0)
    for half in range(2):
        acc = acc_ref[half]
        part_ref[pl.ds(half * TILE, 64), :] = acc[:64, :TILE].astype(BF16)
        part_ref[pl.ds(half * TILE + 64, 64), :] = acc[64:TILE, TILE:].astype(BF16)
    spans = [(head // 2, slice((head % 2) * TILE, (head % 2 + 1) * TILE)) for head in range(HEADS)]
    rows = [tops[half][:, lanes] for half, lanes in spans]
    rows += [acc_ref[half, pl.ds(TILE, 1), lanes] for half, lanes in spans]
    left = jnp.concatenate(rows, axis=0)
    pieces = []
    for _ in range(4):
        piece = left.astype(BF16)
        pieces.append(piece)
        left = left - piece.astype(F32)
    part_ref[pl.ds(256, 32), :] = jnp.concatenate(pieces, axis=0)


def join_kernel(first_ref, second_ref, wk_ref, wv_ref, near_keys, near_values, key_ref, value_ref, sem):
    copies = [
        pltpu.make_async_copy(near_keys, key_ref.at[pl.ds(0, 16)], sem.at[0]),
        pltpu.make_async_copy(near_values, value_ref.at[pl.ds(0, 16)], sem.at[1]),
    ]
    for copy in copies:
        copy.start()
    project_rows(first_ref, second_ref, wk_ref[...], wv_ref[...], key_ref, value_ref, 16)
    for copy in copies:
        copy.wait()


def join(first, second, w_key, wv_t, keys, values):
    vm = pl.BlockSpec(memory_space=VM)
    return pl.pallas_call(
        join_kernel,
        in_specs=[vm] * 6,
        out_specs=[vm] * 2,
        out_shape=[
            jax.ShapeDtypeStruct((32, TILE, 256), BF16),
            jax.ShapeDtypeStruct((32, 2, VROWS, TILE), BF16),
        ],
        scratch_shapes=[pltpu.SemaphoreType.DMA((2,))],
        compiler_params=pltpu.CompilerParams(vmem_limit_bytes=4 << 20),
        cost_estimate=pl.CostEstimate(flops=1 << 29, bytes_accessed=4 << 20, transcendentals=0),
        name="join",
    )(first, second, w_key, wv_t, keys, values)


def attend(group, lists, bias, queries, keys, values):
    vm = pl.BlockSpec(memory_space=VM)
    sm = pl.BlockSpec(memory_space=SM)
    return pl.pallas_call(
        functools.partial(attend_rows, group),
        in_specs=[sm] * 3 + [vm] * 4,
        out_specs=vm,
        out_shape=jax.ShapeDtypeStruct((288, TILE), BF16),
        scratch_shapes=[VM((2, VROWS, PAIR), F32), VM((36, 2, TILE, PAIR), F32)],
        compiler_params=pltpu.CompilerParams(vmem_limit_bytes=14 << 20),
        cost_estimate=pl.CostEstimate(flops=1 << 30, bytes_accessed=8 << 20, transcendentals=1 << 20),
    )(*lists, bias, queries, keys, values)


def finish_kernel(part0, part1, part2, part3, tangent_ref, own_ref, self_ref, wo_ref, gain_ref, out_ref):
    parts = (part0, part1, part2, part3)
    tangent = tangent_ref[...]
    vt = own_ref[...].astype(F32)
    stats = []
    for cell in range(4):
        pieces = parts[cell][pl.ds(256, 32), :].astype(F32)
        stats.append(pieces[:8] + pieces[8:16] + pieces[16:24] + pieces[24:])
    mixed = []
    for head in range(HEADS):
        rows = slice(head * 64, head * 64 + 64)
        own = self_ref[pl.ds(head, 1), :]
        tops = [stat[head : head + 1] for stat in stats]
        top = own
        for other in tops:
            top = jnp.maximum(top, other)
        own_exp = jnp.exp(own - top)
        total = own_exp
        weighted = own_exp.astype(BF16).astype(F32) * vt[rows]
        for cell in range(4):
            factor = jnp.exp(tops[cell] - top)
            total += stats[cell][4 + head : 5 + head] * factor
            weighted += parts[cell][pl.ds(head * 64, 64), :].astype(F32) * factor
        mixed.append((weighted / total).astype(BF16))
    mixed = jnp.concatenate(mixed, axis=0)
    shifted = tangent.astype(F32) + lax.dot_general(
        mixed, wo_ref[...], (((0,), (0,)), ((), ())), preferred_element_type=F32
    )
    normed = shifted / jnp.sqrt(jnp.mean(shifted * shifted, axis=-1, keepdims=True) + 1e-06) * gain_ref[...]
    radius = jnp.sqrt(jnp.sum(normed * normed, axis=-1, keepdims=True) + 1e-06)
    ratio = radius / 16.0
    square = ratio * ratio
    series = ratio * (
        1.0 + square / 6.0 * (1.0 + square / 20.0 * (1.0 + square / 42.0 * (1.0 + square / 72.0)))
    )
    plain = 0.5 * (jnp.exp(ratio) - jnp.exp(-ratio))
    stretched = jnp.where(ratio < 0.75, series, plain)
    out_ref[...] = (16.0 * stretched * normed / radius).astype(BF16)


def finish(parts, tangent, own, self_score, w_out, gain):
    vm = pl.BlockSpec(memory_space=VM)
    return pl.pallas_call(
        finish_kernel,
        in_specs=[vm] * 9,
        out_specs=vm,
        out_shape=jax.ShapeDtypeStruct(tangent.shape, BF16),
        compiler_params=pltpu.CompilerParams(vmem_limit_bytes=8 << 20),
        cost_estimate=pl.CostEstimate(flops=1 << 26, bytes_accessed=1 << 20, transcendentals=1 << 12),
        name="finish",
    )(*parts, tangent, own, self_score, w_out, gain)


def swap(value, axis, size, mask):
    return lax.ppermute(value, axis, [(at, at ^ mask) for at in range(size)])


def grow(value, axis, size, mask):
    return jnp.concatenate([value, swap(value, axis, size, mask)], axis=0)


def per_device(points, w_query, w_key, w_value, w_out, gain, cell_counts, tile_slots, edge_masks):
    me_dst = lax.axis_index("dst")
    me_src = lax.axis_index("src")
    meta = jnp.stack([me_dst, me_src, cell_counts[0, 0]]).astype(jnp.int32)
    tangent = log_map(points)
    first, second, block = tangent[:64], tangent[64:], tangent
    for hop, (one, other) in enumerate(((2, 8), (6, 24), (8, 2), (24, 6))):
        new_first = grow(first, "dst", 32, one)
        second = grow(second, "dst", 32, other)
        first = new_first
        if hop < 2:
            block = grow(block, "src", 4, (1, 3)[hop])
            first, second, block = lax.optimization_barrier((first, second, block))
    far_first = swap(first, "dst", 32, 1)
    far_second = swap(second, "dst", 32, 1)
    bias, *lists = prepare(meta, tile_slots[0, 0], edge_masks[0, 0])
    keys, values, queries, wv_t, own, self_score = project(
        first, second, block.reshape(4, TILE, 256), w_query, w_key, w_value
    )
    keys, values = join(far_first, far_second, w_key, wv_t, keys, values)
    parts = []
    for group, mask in ((3, 2), (2, 3), (1, 1), (0, 0)):
        part = attend(group, lists, bias, queries, keys, values)
        if group:
            part = swap(part, "src", 4, mask)
        parts.append(part)
    return finish(parts, tangent, own, self_score, w_out, gain[None, :])


def solution(mesh):
    return jax.shard_map(
        per_device,
        mesh=mesh,
        in_specs=(
            P(("dst", "src"), None),
            P(),
            P(),
            P(),
            P(),
            P(),
            P("dst", "src"),
            P("dst", "src", None),
            P("dst", "src", None, None, None),
        ),
        out_specs=P(("dst", "src"), None),
        check_vma=False,
    )
```

```python
import functools

import jax
import jax.numpy as jnp
from jax import lax
from jax.experimental import pallas as pl
from jax.experimental.pallas import tpu as pltpu
from jax.sharding import PartitionSpec as P


HEADS = 4
TILE = 128
PAIR = 2 * TILE
VROWS = TILE + 16
MASKED = -1e30
FLOOR = -1e29
PREP = 8
QUAD = 4
OCT = 8
STRIDE = 40
F32 = jnp.float32
BF16 = jnp.bfloat16
VM = pltpu.VMEM
SM = pltpu.SMEM


def inverse_sinh(ratio):
    return jnp.log(ratio + jnp.sqrt(ratio * ratio + 1.0))


def tangent_kernel(points_ref, out_ref):
    values = points_ref[...].astype(F32)
    radius = jnp.sqrt(jnp.sum(values * values, axis=-1, keepdims=True) + 1e-06)
    ratio = radius / 16.0
    out_ref[...] = (16.0 * inverse_sinh(ratio) * values / radius).astype(BF16)


def log_map(points):
    vm = pl.BlockSpec(memory_space=VM)
    return pl.pallas_call(
        tangent_kernel,
        in_specs=[vm],
        out_specs=vm,
        out_shape=jax.ShapeDtypeStruct(points.shape, BF16),
        compiler_params=pltpu.CompilerParams(vmem_limit_bytes=2 << 20),
        cost_estimate=pl.CostEstimate(flops=1 << 18, bytes_accessed=1 << 17, transcendentals=1 << 9),
        name="tangent",
    )(points)


def gray(delta):
    return delta ^ (delta >> 1)


def prep_kernel(live_ref, codes, mask_hbm, bias_hbm, tile_out, count_out, mask_ref, bias_ref, sem, out_sem):
    spare = mask_hbm.shape[0]
    live = live_ref[0]

    def fetch(trip):
        span = pl.ds(trip * PREP, PREP)
        return pltpu.make_async_copy(mask_hbm.at[span], mask_ref.at[span], sem.at[trip])

    def store(trip):
        span = pl.ds(trip * PREP, PREP)
        return pltpu.make_async_copy(bias_ref.at[span], bias_hbm.at[span], out_sem.at[trip])

    last = pltpu.make_async_copy(bias_ref.at[pl.ds(spare, 1)], bias_hbm.at[pl.ds(spare, 1)], out_sem.at[spare // PREP])
    for trip in range(spare // PREP):
        fetch(trip).start()
    row = lax.broadcasted_iota(jnp.int32, (TILE, TILE), 0)
    lane = lax.broadcasted_iota(jnp.int32, (TILE, TILE), 1)
    eye = jnp.where(row == lane, 1.0, 0.0).astype(BF16)
    bias_ref[spare] = jnp.full((TILE, TILE), MASKED, BF16)
    last.start()
    for group in range(4):
        count_out[group] = 0

    def step(trip, _):
        fetch(trip).wait()
        for member in range(PREP):
            slot = trip * PREP + member
            group = codes[slot]
            is_live = slot < live
            at = count_out[group]
            tile_out[jnp.where(is_live, group * STRIDE + at, 4 * STRIDE)] = slot
            count_out[group] = jnp.where(is_live, at + 1, at)
            wanted = jnp.where(is_live, 1, 2)
            bias = jnp.where(mask_ref[slot] == wanted, 0.0, MASKED).astype(BF16)
            bias_ref[slot] = nt_dot(eye, bias).astype(BF16)
        store(trip).start()
        return 0

    lax.fori_loop(0, spare // PREP, step, 0)
    for group in range(4):
        for extra in range(QUAD):
            tile_out[group * STRIDE + count_out[group] + extra] = spare
    for trip in range(spare // PREP):
        store(trip).wait()
    last.wait()


def prepare(live, codes, masks):
    tiles = masks.shape[0]
    vm = pl.BlockSpec(memory_space=VM)
    sm = pl.BlockSpec(memory_space=SM)
    return pl.pallas_call(
        prep_kernel,
        in_specs=[sm, sm, pl.BlockSpec(memory_space=pltpu.HBM)],
        out_specs=[pl.BlockSpec(memory_space=pltpu.HBM), sm, sm],
        out_shape=[
            jax.ShapeDtypeStruct((tiles + 1, TILE, TILE), BF16),
            jax.ShapeDtypeStruct((4 * STRIDE + 8,), jnp.int32),
            jax.ShapeDtypeStruct((4,), jnp.int32),
        ],
        scratch_shapes=[
            VM(masks.shape, jnp.int32),
            VM((tiles + 1, TILE, TILE), BF16),
            pltpu.SemaphoreType.DMA((tiles // PREP,)),
            pltpu.SemaphoreType.DMA((tiles // PREP + 1,)),
        ],
        compiler_params=pltpu.CompilerParams(vmem_limit_bytes=61000000),
        cost_estimate=pl.CostEstimate(flops=1 << 20, bytes_accessed=6 << 20, transcendentals=0),
        name="prep",
    )(live, codes, masks)


def nt_dot(left, right):
    return lax.dot_general(left, right, (((1,), (1,)), ((), ())), preferred_element_type=F32)


def project_rows(first_ref, second_ref, wk, wv, key_ref, value_ref, base):
    ones = jnp.ones((VROWS - TILE, TILE), BF16)

    @pl.loop(0, 4, unroll=True)
    def _(step):
        rows = []
        turned = (step & 1) * 2 + (step >> 1)
        for member in range(4):
            rows.append(first_ref[pl.ds(pl.multiple_of((step * 4 + member) * 64, 64), 64), :])
            rows.append(second_ref[pl.ds(pl.multiple_of((turned * 4 + member) * 64, 64), 64), :])
        rows = jnp.concatenate(rows, axis=0)
        keys = jnp.dot(rows, wk, preferred_element_type=F32).astype(BF16)
        values = nt_dot(wv, rows).astype(BF16)
        for member in range(4):
            at = base + step * 4 + member
            span = slice(member * TILE, (member + 1) * TILE)
            key_ref[at] = keys[span]
            for half in range(2):
                value_ref[at, half, pl.ds(0, TILE), :] = values[half * TILE : (half + 1) * TILE, span]
                value_ref[at, half, pl.ds(TILE, VROWS - TILE), :] = ones


def project_kernel(
    first_ref, second_ref, block_ref, wq_ref, wk_ref, wv_ref, key_ref, value_ref, query_ref, turned_ref, own_ref, self_ref
):
    wq, wk = wq_ref[...], wk_ref[...]
    wv_t = wv_ref[...].astype(F32).T.astype(BF16)
    turned_ref[...] = wv_t
    wq_t = wq.astype(F32).T.astype(BF16)
    zero = jnp.zeros((64, TILE), BF16)
    for group in range(4):
        qt = nt_dot(wq_t, block_ref[group]).astype(BF16).astype(F32) * 0.125
        low = qt.astype(BF16)
        for half in range(2):
            upper = jnp.concatenate([low[half * TILE : half * TILE + 64], zero], axis=1)
            lower = jnp.concatenate([zero, low[half * TILE + 64 : half * TILE + TILE]], axis=1)
            query_ref[group, half] = jnp.concatenate([upper, lower], axis=0)
        if group == 0:
            wk_t = wk.astype(F32).T.astype(BF16)
            product = qt * nt_dot(wk_t, block_ref[0]).astype(BF16).astype(F32)
            for head in range(HEADS):
                total = jnp.sum(product[head * 64 : (head + 1) * 64], axis=0, keepdims=True)
                self_ref[pl.ds(head, 1), :] = total
            own_ref[...] = nt_dot(wv_t, block_ref[0]).astype(BF16)
    project_rows(first_ref, second_ref, wk, wv_t, key_ref, value_ref, 0)


def project(first, second, block, w_query, w_key, w_value):
    vm = pl.BlockSpec(memory_space=VM)
    return pl.pallas_call(
        project_kernel,
        in_specs=[vm] * 6,
        out_specs=[vm] * 6,
        out_shape=[
            jax.ShapeDtypeStruct((16, TILE, 256), BF16),
            jax.ShapeDtypeStruct((16, 2, VROWS, TILE), BF16),
            jax.ShapeDtypeStruct((4, 2, TILE, PAIR), BF16),
            jax.ShapeDtypeStruct((256, 256), BF16),
            jax.ShapeDtypeStruct((256, TILE), BF16),
            jax.ShapeDtypeStruct((HEADS, TILE), F32),
        ],
        compiler_params=pltpu.CompilerParams(vmem_limit_bytes=8 << 20),
        cost_estimate=pl.CostEstimate(flops=1 << 29, bytes_accessed=4 << 20, transcendentals=0),
        name="project",
    )(first, second, block, w_query, w_key, w_value)


def attend_rows(
    group, spot_list, tile_list, counts, bias_ref, query_ref, key_ref, value_ref, part_ref, acc_ref, score_ref
):
    base = group * STRIDE
    count = counts[group]
    most = count // OCT
    quads = (count - most * OCT + 1) // QUAD
    quad_at = most * OCT
    rest_at = quad_at + quads * QUAD
    rest = (count - rest_at + 1) // 2

    def score(start, size, tops):
        tops = list(tops)
        names = [tile_list[base + start + member] for member in range(size)]
        spots = [spot_list[name] for name in names]
        for half in range(2):
            keys = jnp.concatenate([key_ref[spot, :, half * TILE : (half + 1) * TILE] for spot in spots], axis=0)
            scores = jnp.dot(keys, query_ref[group, half], preferred_element_type=F32)
            for member in range(size):
                bias = bias_ref[names[member]].astype(F32)
                part = scores[member * TILE : (member + 1) * TILE] + jnp.concatenate([bias, bias], axis=1)
                score_ref[start + member, half] = part
                tops[half] = jnp.maximum(tops[half], jnp.max(part.reshape(16, 8, PAIR), axis=0))
        return tuple(tops)

    floor = jnp.full((8, PAIR), FLOOR, F32)
    tops = lax.fori_loop(0, most, lambda trip, tops: score(trip * OCT, OCT, tops), (floor, floor))
    tops = lax.fori_loop(0, quads, lambda trip, tops: score(quad_at + trip * QUAD, QUAD, tops), tops)
    tops = lax.fori_loop(0, rest, lambda trip, tops: score(rest_at + trip * 2, 2, tops), tops)
    tops = [jnp.max(top, axis=0, keepdims=True) for top in tops]
    acc_ref[...] = jnp.zeros(acc_ref.shape, F32)

    def mix(start, size):
        spots = [spot_list[tile_list[base + start + member]] for member in range(size)]
        for half in range(2):
            weights = [jnp.exp(score_ref[start + member, half] - tops[half]).astype(BF16) for member in range(size)]
            values = jnp.concatenate([value_ref[spot, half] for spot in spots], axis=1)
            acc_ref[half] += jnp.dot(values, jnp.concatenate(weights, axis=0), preferred_element_type=F32)
        return 0

    lax.fori_loop(0, most, lambda trip, _: mix(trip * OCT, OCT), 0)
    lax.fori_loop(0, quads, lambda trip, _: mix(quad_at + trip * QUAD, QUAD), 0)
    lax.fori_loop(0, rest, lambda trip, _: mix(rest_at + trip * 2, 2), 0)
    for half in range(2):
        acc = acc_ref[half]
        part_ref[pl.ds(half * TILE, 64), :] = acc[:64, :TILE].astype(BF16)
        part_ref[pl.ds(half * TILE + 64, 64), :] = acc[64:TILE, TILE:].astype(BF16)
    spans = [(head // 2, slice((head % 2) * TILE, (head % 2 + 1) * TILE)) for head in range(HEADS)]
    rows = [tops[half][:, lanes] for half, lanes in spans]
    rows += [acc_ref[half, pl.ds(TILE, 1), lanes] for half, lanes in spans]
    left = jnp.concatenate(rows, axis=0)
    pieces = []
    for _ in range(4):
        piece = left.astype(BF16)
        pieces.append(piece)
        left = left - piece.astype(F32)
    part_ref[pl.ds(256, 32), :] = jnp.concatenate(pieces, axis=0)


def join_kernel(first_ref, second_ref, wk_ref, wv_ref, near_keys, near_values, key_ref, value_ref, sem):
    copies = [
        pltpu.make_async_copy(near_keys, key_ref.at[pl.ds(0, 16)], sem.at[0]),
        pltpu.make_async_copy(near_values, value_ref.at[pl.ds(0, 16)], sem.at[1]),
    ]
    for copy in copies:
        copy.start()
    project_rows(first_ref, second_ref, wk_ref[...], wv_ref[...], key_ref, value_ref, 16)
    for copy in copies:
        copy.wait()


def join(first, second, w_key, wv_t, keys, values):
    vm = pl.BlockSpec(memory_space=VM)
    return pl.pallas_call(
        join_kernel,
        in_specs=[vm] * 6,
        out_specs=[vm] * 2,
        out_shape=[
            jax.ShapeDtypeStruct((32, TILE, 256), BF16),
            jax.ShapeDtypeStruct((32, 2, VROWS, TILE), BF16),
        ],
        scratch_shapes=[pltpu.SemaphoreType.DMA((2,))],
        compiler_params=pltpu.CompilerParams(vmem_limit_bytes=4 << 20),
        cost_estimate=pl.CostEstimate(flops=1 << 29, bytes_accessed=4 << 20, transcendentals=0),
        name="join",
    )(first, second, w_key, wv_t, keys, values)


def attend(group, lists, bias, queries, keys, values):
    vm = pl.BlockSpec(memory_space=VM)
    sm = pl.BlockSpec(memory_space=SM)
    return pl.pallas_call(
        functools.partial(attend_rows, group),
        in_specs=[sm] * 3 + [vm] * 4,
        out_specs=vm,
        out_shape=jax.ShapeDtypeStruct((288, TILE), BF16),
        scratch_shapes=[VM((2, VROWS, PAIR), F32), VM((36, 2, TILE, PAIR), F32)],
        compiler_params=pltpu.CompilerParams(vmem_limit_bytes=14 << 20),
        cost_estimate=pl.CostEstimate(flops=1 << 30, bytes_accessed=8 << 20, transcendentals=1 << 20),
    )(*lists, bias, queries, keys, values)


def finish_kernel(part0, part1, part2, part3, tangent_ref, own_ref, self_ref, wo_ref, gain_ref, out_ref):
    parts = (part0, part1, part2, part3)
    tangent = tangent_ref[...]
    vt = own_ref[...].astype(F32)
    stats = []
    for cell in range(4):
        pieces = parts[cell][pl.ds(256, 32), :].astype(F32)
        stats.append(pieces[:8] + pieces[8:16] + pieces[16:24] + pieces[24:])
    mixed = []
    for head in range(HEADS):
        rows = slice(head * 64, head * 64 + 64)
        own = self_ref[pl.ds(head, 1), :]
        tops = [stat[head : head + 1] for stat in stats]
        top = own
        for other in tops:
            top = jnp.maximum(top, other)
        own_exp = jnp.exp(own - top)
        total = own_exp
        weighted = own_exp.astype(BF16).astype(F32) * vt[rows]
        for cell in range(4):
            factor = jnp.exp(tops[cell] - top)
            total += stats[cell][4 + head : 5 + head] * factor
            weighted += parts[cell][pl.ds(head * 64, 64), :].astype(F32) * factor
        mixed.append((weighted / total).astype(BF16))
    mixed = jnp.concatenate(mixed, axis=0)
    shifted = tangent.astype(F32) + lax.dot_general(
        mixed, wo_ref[...], (((0,), (0,)), ((), ())), preferred_element_type=F32
    )
    normed = shifted / jnp.sqrt(jnp.mean(shifted * shifted, axis=-1, keepdims=True) + 1e-06) * gain_ref[...]
    radius = jnp.sqrt(jnp.sum(normed * normed, axis=-1, keepdims=True) + 1e-06)
    ratio = radius / 16.0
    square = ratio * ratio
    series = ratio * (
        1.0 + square / 6.0 * (1.0 + square / 20.0 * (1.0 + square / 42.0 * (1.0 + square / 72.0)))
    )
    plain = 0.5 * (jnp.exp(ratio) - jnp.exp(-ratio))
    stretched = jnp.where(ratio < 0.75, series, plain)
    out_ref[...] = (16.0 * stretched * normed / radius).astype(BF16)


def finish(parts, tangent, own, self_score, w_out, gain):
    vm = pl.BlockSpec(memory_space=VM)
    return pl.pallas_call(
        finish_kernel,
        in_specs=[vm] * 9,
        out_specs=vm,
        out_shape=jax.ShapeDtypeStruct(tangent.shape, BF16),
        compiler_params=pltpu.CompilerParams(vmem_limit_bytes=8 << 20),
        cost_estimate=pl.CostEstimate(flops=1 << 26, bytes_accessed=1 << 20, transcendentals=1 << 12),
        name="finish",
    )(*parts, tangent, own, self_score, w_out, gain)


def swap(value, axis, size, mask):
    return lax.ppermute(value, axis, [(at, at ^ mask) for at in range(size)])


def grow(value, axis, size, mask):
    return jnp.concatenate([value, swap(value, axis, size, mask)], axis=0)


def per_device(points, w_query, w_key, w_value, w_out, gain, cell_counts, tile_slots, edge_masks):
    me_dst = lax.axis_index("dst")
    me_src = lax.axis_index("src")
    named = tile_slots[0, 0]
    codes = gray((named >> 5) ^ me_src)
    delta = (named & 31) ^ me_dst
    along_x, along_y = gray((delta >> 1) & 3), gray((delta >> 3) & 3)
    spots = (delta & 1) * 16 + (along_y >> 1) * 8 + (along_x >> 1) * 4 + (along_y & 1) * 2 + (along_x & 1)
    spots = jnp.concatenate([spots, jnp.zeros((8,), jnp.int32)])
    tangent = log_map(points)
    near = swap(tangent, "dst", 32, 2)
    block = grow(tangent, "src", 4, 1)
    near = jnp.concatenate([tangent[:64], near[:64], tangent[64:], near[64:]], axis=0)
    next_near = swap(near, "dst", 32, 8)
    block = grow(block, "src", 4, 3)
    first = jnp.concatenate([near[:128], next_near[:128]], axis=0)
    second = jnp.concatenate([near[128:], next_near[128:]], axis=0)
    first, second = lax.optimization_barrier((first, second))
    for (one, other) in ((6, 24), (24, 6)):
        new_first = grow(first, "dst", 32, one)
        second = grow(second, "dst", 32, other)
        first = new_first
    far_first = swap(first, "dst", 32, 1)
    far_second = swap(second, "dst", 32, 1)
    bias, *lists = prepare(cell_counts[0], codes, edge_masks[0, 0])
    keys, values, queries, wv_t, own, self_score = project(
        first, second, block.reshape(4, TILE, 256), w_query, w_key, w_value
    )
    keys, values = join(far_first, far_second, w_key, wv_t, keys, values)
    parts = []
    for group, mask in ((3, 2), (2, 3), (1, 1), (0, 0)):
        part = attend(group, (spots, *lists), bias, queries, keys, values)
        if group:
            part = swap(part, "src", 4, mask)
        parts.append(part)
    return finish(parts, tangent, own, self_score, w_out, gain[None, :])


def solution(mesh):
    return jax.shard_map(
        per_device,
        mesh=mesh,
        in_specs=(
            P(("dst", "src"), None),
            P(),
            P(),
            P(),
            P(),
            P(),
            P("dst", "src"),
            P("dst", "src", None),
            P("dst", "src", None, None, None),
        ),
        out_specs=P(("dst", "src"), None),
        check_vma=False,
    )
```

```python
import functools

import jax
import jax.numpy as jnp
from jax import lax
from jax.experimental import pallas as pl
from jax.experimental.pallas import tpu as pltpu
from jax.sharding import PartitionSpec as P


HEADS = 4
TILE = 128
PAIR = 2 * TILE
VROWS = TILE + 16
MASKED = -1e30
FLOOR = -1e29
PREP = 8
QUAD = 4
STRIDE = 40
F32 = jnp.float32
BF16 = jnp.bfloat16
VM = pltpu.VMEM
SM = pltpu.SMEM


def inverse_sinh(ratio):
    return jnp.log(ratio + jnp.sqrt(ratio * ratio + 1.0))


def tangent_kernel(points_ref, out_ref):
    values = points_ref[...].astype(F32)
    radius = jnp.sqrt(jnp.sum(values * values, axis=-1, keepdims=True) + 1e-06)
    ratio = radius / 16.0
    out_ref[...] = (16.0 * inverse_sinh(ratio) * values / radius).astype(BF16)


def log_map(points):
    vm = pl.BlockSpec(memory_space=VM)
    return pl.pallas_call(
        tangent_kernel,
        in_specs=[vm],
        out_specs=vm,
        out_shape=jax.ShapeDtypeStruct(points.shape, BF16),
        compiler_params=pltpu.CompilerParams(vmem_limit_bytes=2 << 20),
        cost_estimate=pl.CostEstimate(flops=1 << 18, bytes_accessed=1 << 17, transcendentals=1 << 9),
        name="tangent",
    )(points)


def gray(delta):
    return delta ^ (delta >> 1)


def prep_kernel(live_ref, codes, mask_hbm, bias_hbm, tile_out, count_out, mask_ref, bias_ref, sem, out_sem):
    spare = mask_hbm.shape[0]
    live = live_ref[0]

    def fetch(trip):
        span = pl.ds(trip * PREP, PREP)
        return pltpu.make_async_copy(mask_hbm.at[span], mask_ref.at[span], sem.at[trip])

    def store(trip):
        span = pl.ds(trip * PREP, PREP)
        return pltpu.make_async_copy(bias_ref.at[span], bias_hbm.at[span], out_sem.at[trip])

    last = pltpu.make_async_copy(bias_ref.at[pl.ds(spare, 1)], bias_hbm.at[pl.ds(spare, 1)], out_sem.at[spare // PREP])
    for trip in range(spare // PREP):
        fetch(trip).start()
    row = lax.broadcasted_iota(jnp.int32, (TILE, TILE), 0)
    lane = lax.broadcasted_iota(jnp.int32, (TILE, TILE), 1)
    eye = jnp.where(row == lane, 1.0, 0.0).astype(BF16)
    bias_ref[spare] = jnp.full((TILE, TILE), MASKED, BF16)
    last.start()
    for group in range(4):
        count_out[group] = 0

    def step(trip, _):
        fetch(trip).wait()
        for member in range(PREP):
            slot = trip * PREP + member
            group = codes[slot]
            is_live = slot < live
            at = count_out[group]
            tile_out[jnp.where(is_live, group * STRIDE + at, 4 * STRIDE)] = slot
            count_out[group] = jnp.where(is_live, at + 1, at)
            wanted = jnp.where(is_live, 1, 2)
            bias = jnp.where(mask_ref[slot] == wanted, 0.0, MASKED).astype(BF16)
            bias_ref[slot] = nt_dot(eye, bias).astype(BF16)
        store(trip).start()
        return 0

    lax.fori_loop(0, spare // PREP, step, 0)
    for group in range(4):
        for extra in range(QUAD):
            tile_out[group * STRIDE + count_out[group] + extra] = spare
    for trip in range(spare // PREP):
        store(trip).wait()
    last.wait()


def prepare(live, codes, masks):
    tiles = masks.shape[0]
    vm = pl.BlockSpec(memory_space=VM)
    sm = pl.BlockSpec(memory_space=SM)
    return pl.pallas_call(
        prep_kernel,
        in_specs=[sm, sm, pl.BlockSpec(memory_space=pltpu.HBM)],
        out_specs=[pl.BlockSpec(memory_space=pltpu.HBM), sm, sm],
        out_shape=[
            jax.ShapeDtypeStruct((tiles + 1, TILE, TILE), BF16),
            jax.ShapeDtypeStruct((4 * STRIDE + 8,), jnp.int32),
            jax.ShapeDtypeStruct((4,), jnp.int32),
        ],
        scratch_shapes=[
            VM(masks.shape, jnp.int32),
            VM((tiles + 1, TILE, TILE), BF16),
            pltpu.SemaphoreType.DMA((tiles // PREP,)),
            pltpu.SemaphoreType.DMA((tiles // PREP + 1,)),
        ],
        compiler_params=pltpu.CompilerParams(vmem_limit_bytes=61000000),
        cost_estimate=pl.CostEstimate(flops=1 << 20, bytes_accessed=6 << 20, transcendentals=0),
        name="prep",
    )(live, codes, masks)


def nt_dot(left, right):
    return lax.dot_general(left, right, (((1,), (1,)), ((), ())), preferred_element_type=F32)


def project_rows(first_ref, second_ref, wk, wv, key_ref, value_ref, base):
    ones = jnp.ones((VROWS - TILE, TILE), BF16)

    @pl.loop(0, 4, unroll=True)
    def _(step):
        rows = []
        turned = (step & 1) * 2 + (step >> 1)
        for member in range(4):
            rows.append(first_ref[pl.ds(pl.multiple_of((step * 4 + member) * 64, 64), 64), :])
            rows.append(second_ref[pl.ds(pl.multiple_of((turned * 4 + member) * 64, 64), 64), :])
        rows = jnp.concatenate(rows, axis=0)
        keys = jnp.dot(rows, wk, preferred_element_type=F32).astype(BF16)
        values = nt_dot(wv, rows).astype(BF16)
        for member in range(4):
            at = base + step * 4 + member
            span = slice(member * TILE, (member + 1) * TILE)
            key_ref[at] = keys[span]
            for half in range(2):
                value_ref[at, half, pl.ds(0, TILE), :] = values[half * TILE : (half + 1) * TILE, span]
                value_ref[at, half, pl.ds(TILE, VROWS - TILE), :] = ones


def project_kernel(
    first_ref, second_ref, block_ref, wq_ref, wk_ref, wv_ref, key_ref, value_ref, query_ref, turned_ref, own_ref, self_ref
):
    wq, wk = wq_ref[...], wk_ref[...]
    wv_t = wv_ref[...].astype(F32).T.astype(BF16)
    turned_ref[...] = wv_t
    wq_t = wq.astype(F32).T.astype(BF16)
    zero = jnp.zeros((64, TILE), BF16)
    for group in range(4):
        qt = nt_dot(wq_t, block_ref[group]).astype(BF16).astype(F32) * 0.125
        low = qt.astype(BF16)
        for half in range(2):
            upper = jnp.concatenate([low[half * TILE : half * TILE + 64], zero], axis=1)
            lower = jnp.concatenate([zero, low[half * TILE + 64 : half * TILE + TILE]], axis=1)
            query_ref[group, half] = jnp.concatenate([upper, lower], axis=0)
        if group == 0:
            wk_t = wk.astype(F32).T.astype(BF16)
            product = qt * nt_dot(wk_t, block_ref[0]).astype(BF16).astype(F32)
            for head in range(HEADS):
                total = jnp.sum(product[head * 64 : (head + 1) * 64], axis=0, keepdims=True)
                self_ref[pl.ds(head, 1), :] = total
            own_ref[...] = nt_dot(wv_t, block_ref[0]).astype(BF16)
    project_rows(first_ref, second_ref, wk, wv_t, key_ref, value_ref, 0)


def project(first, second, block, w_query, w_key, w_value):
    vm = pl.BlockSpec(memory_space=VM)
    return pl.pallas_call(
        project_kernel,
        in_specs=[vm] * 6,
        out_specs=[vm] * 6,
        out_shape=[
            jax.ShapeDtypeStruct((16, TILE, 256), BF16),
            jax.ShapeDtypeStruct((16, 2, VROWS, TILE), BF16),
            jax.ShapeDtypeStruct((4, 2, TILE, PAIR), BF16),
            jax.ShapeDtypeStruct((256, 256), BF16),
            jax.ShapeDtypeStruct((256, TILE), BF16),
            jax.ShapeDtypeStruct((HEADS, TILE), F32),
        ],
        compiler_params=pltpu.CompilerParams(vmem_limit_bytes=8 << 20),
        cost_estimate=pl.CostEstimate(flops=1 << 29, bytes_accessed=4 << 20, transcendentals=0),
        name="project",
    )(first, second, block, w_query, w_key, w_value)


def attend_rows(
    group, spot_list, tile_list, counts, bias_ref, query_ref, key_ref, value_ref, part_ref, acc_ref, score_ref
):
    base = group * STRIDE
    count = counts[group]
    ladder = []
    done = jnp.int32(0)
    for size in (16, 8, 4, 2):
        pad = 1 if size <= QUAD else 0
        trips = (count - done + pad) // size
        ladder.append((size, done, trips))
        done = done + trips * size

    def score(start, size, tops):
        tops = list(tops)
        names = [tile_list[base + start + member] for member in range(size)]
        spots = [spot_list[name] for name in names]
        for half in range(2):
            keys = jnp.concatenate([key_ref[spot, :, half * TILE : (half + 1) * TILE] for spot in spots], axis=0)
            scores = jnp.dot(keys, query_ref[group, half], preferred_element_type=F32)
            for member in range(size):
                bias = bias_ref[names[member]].astype(F32)
                part = scores[member * TILE : (member + 1) * TILE] + jnp.concatenate([bias, bias], axis=1)
                score_ref[start + member, half] = part
                tops[half] = jnp.maximum(tops[half], jnp.max(part.reshape(16, 8, PAIR), axis=0))
        return tuple(tops)

    floor = jnp.full((8, PAIR), FLOOR, F32)
    tops = (floor, floor)
    for size, start, trips in ladder:
        tops = lax.fori_loop(0, trips, lambda trip, tops: score(start + trip * size, size, tops), tops)
    tops = [jnp.max(top, axis=0, keepdims=True) for top in tops]
    acc_ref[...] = jnp.zeros(acc_ref.shape, F32)

    def mix(start, size):
        spots = [spot_list[tile_list[base + start + member]] for member in range(size)]
        for half in range(2):
            weights = [jnp.exp(score_ref[start + member, half] - tops[half]).astype(BF16) for member in range(size)]
            values = jnp.concatenate([value_ref[spot, half] for spot in spots], axis=1)
            acc_ref[half] += jnp.dot(values, jnp.concatenate(weights, axis=0), preferred_element_type=F32)
        return 0

    for size, start, trips in ladder:
        lax.fori_loop(0, trips, lambda trip, _: mix(start + trip * size, size), 0)
    for half in range(2):
        acc = acc_ref[half]
        part_ref[pl.ds(half * TILE, 64), :] = acc[:64, :TILE].astype(BF16)
        part_ref[pl.ds(half * TILE + 64, 64), :] = acc[64:TILE, TILE:].astype(BF16)
    spans = [(head // 2, slice((head % 2) * TILE, (head % 2 + 1) * TILE)) for head in range(HEADS)]
    rows = [tops[half][:, lanes] for half, lanes in spans]
    rows += [acc_ref[half, pl.ds(TILE, 1), lanes] for half, lanes in spans]
    left = jnp.concatenate(rows, axis=0)
    pieces = []
    for _ in range(4):
        piece = left.astype(BF16)
        pieces.append(piece)
        left = left - piece.astype(F32)
    part_ref[pl.ds(256, 32), :] = jnp.concatenate(pieces, axis=0)


def join_kernel(first_ref, second_ref, wk_ref, wv_ref, near_keys, near_values, key_ref, value_ref, sem):
    copies = [
        pltpu.make_async_copy(near_keys, key_ref.at[pl.ds(0, 16)], sem.at[0]),
        pltpu.make_async_copy(near_values, value_ref.at[pl.ds(0, 16)], sem.at[1]),
    ]
    for copy in copies:
        copy.start()
    project_rows(first_ref, second_ref, wk_ref[...], wv_ref[...], key_ref, value_ref, 16)
    for copy in copies:
        copy.wait()


def join(first, second, w_key, wv_t, keys, values):
    vm = pl.BlockSpec(memory_space=VM)
    return pl.pallas_call(
        join_kernel,
        in_specs=[vm] * 6,
        out_specs=[vm] * 2,
        out_shape=[
            jax.ShapeDtypeStruct((32, TILE, 256), BF16),
            jax.ShapeDtypeStruct((32, 2, VROWS, TILE), BF16),
        ],
        scratch_shapes=[pltpu.SemaphoreType.DMA((2,))],
        compiler_params=pltpu.CompilerParams(vmem_limit_bytes=4 << 20),
        cost_estimate=pl.CostEstimate(flops=1 << 29, bytes_accessed=4 << 20, transcendentals=0),
        name="join",
    )(first, second, w_key, wv_t, keys, values)


def attend(group, lists, bias, queries, keys, values):
    vm = pl.BlockSpec(memory_space=VM)
    sm = pl.BlockSpec(memory_space=SM)
    return pl.pallas_call(
        functools.partial(attend_rows, group),
        in_specs=[sm] * 3 + [vm] * 4,
        out_specs=vm,
        out_shape=jax.ShapeDtypeStruct((288, TILE), BF16),
        scratch_shapes=[VM((2, VROWS, PAIR), F32), VM((36, 2, TILE, PAIR), F32)],
        compiler_params=pltpu.CompilerParams(vmem_limit_bytes=14 << 20),
        cost_estimate=pl.CostEstimate(flops=1 << 30, bytes_accessed=8 << 20, transcendentals=1 << 20),
    )(*lists, bias, queries, keys, values)


def finish_kernel(part0, part1, part2, part3, tangent_ref, own_ref, self_ref, wo_ref, gain_ref, out_ref):
    parts = (part0, part1, part2, part3)
    tangent = tangent_ref[...]
    vt = own_ref[...].astype(F32)
    stats = []
    for cell in range(4):
        pieces = parts[cell][pl.ds(256, 32), :].astype(F32)
        stats.append(pieces[:8] + pieces[8:16] + pieces[16:24] + pieces[24:])
    mixed = []
    for head in range(HEADS):
        rows = slice(head * 64, head * 64 + 64)
        own = self_ref[pl.ds(head, 1), :]
        tops = [stat[head : head + 1] for stat in stats]
        top = own
        for other in tops:
            top = jnp.maximum(top, other)
        own_exp = jnp.exp(own - top)
        total = own_exp
        weighted = own_exp.astype(BF16).astype(F32) * vt[rows]
        for cell in range(4):
            factor = jnp.exp(tops[cell] - top)
            total += stats[cell][4 + head : 5 + head] * factor
            weighted += parts[cell][pl.ds(head * 64, 64), :].astype(F32) * factor
        mixed.append((weighted / total).astype(BF16))
    mixed = jnp.concatenate(mixed, axis=0)
    shifted = tangent.astype(F32) + lax.dot_general(
        mixed, wo_ref[...], (((0,), (0,)), ((), ())), preferred_element_type=F32
    )
    normed = shifted / jnp.sqrt(jnp.mean(shifted * shifted, axis=-1, keepdims=True) + 1e-06) * gain_ref[...]
    radius = jnp.sqrt(jnp.sum(normed * normed, axis=-1, keepdims=True) + 1e-06)
    ratio = radius / 16.0
    square = ratio * ratio
    series = ratio * (
        1.0 + square / 6.0 * (1.0 + square / 20.0 * (1.0 + square / 42.0 * (1.0 + square / 72.0)))
    )
    plain = 0.5 * (jnp.exp(ratio) - jnp.exp(-ratio))
    stretched = jnp.where(ratio < 0.75, series, plain)
    out_ref[...] = (16.0 * stretched * normed / radius).astype(BF16)


def finish(parts, tangent, own, self_score, w_out, gain):
    vm = pl.BlockSpec(memory_space=VM)
    return pl.pallas_call(
        finish_kernel,
        in_specs=[vm] * 9,
        out_specs=vm,
        out_shape=jax.ShapeDtypeStruct(tangent.shape, BF16),
        compiler_params=pltpu.CompilerParams(vmem_limit_bytes=8 << 20),
        cost_estimate=pl.CostEstimate(flops=1 << 26, bytes_accessed=1 << 20, transcendentals=1 << 12),
        name="finish",
    )(*parts, tangent, own, self_score, w_out, gain)


def swap(value, axis, size, mask):
    return lax.ppermute(value, axis, [(at, at ^ mask) for at in range(size)])


def grow(value, axis, size, mask):
    return jnp.concatenate([value, swap(value, axis, size, mask)], axis=0)


def per_device(points, w_query, w_key, w_value, w_out, gain, cell_counts, tile_slots, edge_masks):
    me_dst = lax.axis_index("dst")
    me_src = lax.axis_index("src")
    named = tile_slots[0, 0]
    codes = gray((named >> 5) ^ me_src)
    delta = (named & 31) ^ me_dst
    along_x, along_y = gray((delta >> 1) & 3), gray((delta >> 3) & 3)
    spots = (delta & 1) * 16 + (along_y >> 1) * 8 + (along_x >> 1) * 4 + (along_y & 1) * 2 + (along_x & 1)
    spots = jnp.concatenate([spots, jnp.zeros((8,), jnp.int32)])
    tangent = log_map(points)
    near = swap(tangent, "dst", 32, 2)
    block = grow(tangent, "src", 4, 1)
    near = jnp.concatenate([tangent[:64], near[:64], tangent[64:], near[64:]], axis=0)
    next_near = swap(near, "dst", 32, 8)
    block = grow(block, "src", 4, 3)
    first = jnp.concatenate([near[:128], next_near[:128]], axis=0)
    second = jnp.concatenate([near[128:], next_near[128:]], axis=0)
    first, second = lax.optimization_barrier((first, second))
    for (one, other) in ((6, 24), (24, 6)):
        new_first = grow(first, "dst", 32, one)
        second = grow(second, "dst", 32, other)
        first = new_first
    far_first = swap(first, "dst", 32, 1)
    far_second = swap(second, "dst", 32, 1)
    bias, *lists = prepare(cell_counts[0], codes, edge_masks[0, 0])
    keys, values, queries, wv_t, own, self_score = project(
        first, second, block.reshape(4, TILE, 256), w_query, w_key, w_value
    )
    keys, values = join(far_first, far_second, w_key, wv_t, keys, values)
    parts = []
    for group, mask in ((3, 2), (2, 3), (1, 1), (0, 0)):
        part = attend(group, (spots, *lists), bias, queries, keys, values)
        if group:
            part = swap(part, "src", 4, mask)
        parts.append(part)
    return finish(parts, tangent, own, self_score, w_out, gain[None, :])


def solution(mesh):
    return jax.shard_map(
        per_device,
        mesh=mesh,
        in_specs=(
            P(("dst", "src"), None),
            P(),
            P(),
            P(),
            P(),
            P(),
            P("dst", "src"),
            P("dst", "src", None),
            P("dst", "src", None, None, None),
        ),
        out_specs=P(("dst", "src"), None),
        check_vma=False,
    )
```
